32 devices in a mesh: gx: 4 (over y, core), gy: 4 (over z), gz: 2 (over x).
Axes of the slice: x: 2, y: 2, z: 4, core: 2. Of those that a mesh axis runs over, the one named last changes fastest.
Arguments:
- w_minus: bfloat16 [4, 4, 2, 3, 512, 1024], P('gx', 'gy', 'gz'), may hold values from -0.25 to 0.25
- w_plus: bfloat16 [4, 4, 2, 3, 512, 1024], P('gx', 'gy', 'gz'), may hold values from -0.25 to 0.25
- interior: bfloat16 [4, 4, 2, 512, 512], P('gx', 'gy', 'gz')
- b_minus: bfloat16 [4, 4, 2, 3, 1024], P('gx', 'gy', 'gz'), may hold values from 2 to 4
- b_plus: bfloat16 [4, 4, 2, 3, 1024], P('gx', 'gy', 'gz'), may hold values from 2 to 4
- walls: int32 [4, 4, 2, 3], P('gx', 'gy', 'gz'), may hold values from 0 to 1, as said below
Outputs:
- assembled: bfloat16 [4, 4, 2, 3, 1024, 1024], P('gx', 'gy', 'gz')
The draws below stay inside these ranges and needn't reach their ends.
Inputs may be any that keep to these rules, and one draw needn't show every extreme that they name: Every subdomain with the last index along axis a has walls 1 for axis a.
All inputs are finite; a program needn't handle non-finite values.
Results may differ from the reference program's by a relative error of at most 0.0039.
Values may be sent and summed in bfloat16 or wider, within the bound.
No kernel may reach another device: no remote copies, remote signals or barrier semaphores. Data moves between devices by JAX's collectives and lax.ppermute only.
A program may use at most 128 MiB of HBM per device.

```python
import jax
import jax.numpy as jnp
from jax import lax

FSIDE = 32
F = 1024
R = 512
NDX = 4
NDY = 4
NDZ = 2


def draw_walls(key, part):
    shape = (NDX, NDY, NDZ, 3)
    raw = jax.random.randint(key, shape, 0, 4)
    flags = (raw == 0).astype(jnp.int32)
    which = lax.broadcasted_iota(jnp.int32, shape, 3)
    at_end = (which == 0) & (lax.broadcasted_iota(jnp.int32, shape, 0) == NDX - 1) | (which == 1) & (lax.broadcasted_iota(jnp.int32, shape, 1) == NDY - 1) | (which == 2) & (lax.broadcasted_iota(jnp.int32, shape, 2) == NDZ - 1)
    return jnp.where(at_end, 1, flags).astype(jnp.int32)


def draw_interior(key, part):
    first = jax.random.fold_in(key, 11)
    second = jax.random.fold_in(key, 12)
    shape = (NDX, NDY, NDZ, R, R)
    spread = jax.random.normal(first, shape, jnp.float32) * (0.5 / R ** 0.5)
    levels = jax.random.uniform(second, (NDX, NDY, NDZ, R), jnp.float32, 0.5, 1.5)
    eye_mask = (lax.broadcasted_iota(jnp.int32, shape, 3) == lax.broadcasted_iota(jnp.int32, shape, 4)).astype(jnp.float32)
    return (spread + eye_mask * levels[..., None]).astype(jnp.bfloat16)


def block_scale(own_key, dims, split, least, top_value):
    def one(dim, parts):
        draws = jax.random.uniform(jax.random.fold_in(jax.random.fold_in(own_key, 6), dim), (parts,), jnp.float32, least / len(split), top_value / len(split))
        return jnp.repeat(jnp.exp(draws), dims[dim] // parts).reshape((-1,) + (1,) * (len(dims) - dim - 1))

    factor_of = one(*split[0])
    for cut in split[1:]:
        factor_of = factor_of * one(*cut)
    return factor_of


def scatter_about(stream_key, shape, scale, bound, shards=(), kind=jnp.bfloat16):
    array = scale * jax.random.normal(stream_key, shape, jnp.float32)
    if shards:
        array = array * block_scale(stream_key, shape, shards, -0.22, 0.18)
    return jnp.clip(array, -bound, bound).astype(kind)


def setup_inputs(seed: int = 0) -> dict:
    splits = jax.random.split(jax.random.key(seed), 7)
    w_minus = scatter_about(splits[0], (NDX, NDY, NDZ, 3, R, F), R ** -0.5, 0.25, ((0, 4), (1, 4), (2, 2)))
    w_plus = scatter_about(splits[1], (NDX, NDY, NDZ, 3, R, F), R ** -0.5, 0.25, ((0, 4), (1, 4), (2, 2)))
    interior = draw_interior(jax.random.fold_in(splits[6], 71), 0)
    b_minus = jnp.clip(2.0 + 2.0 * jax.random.uniform(splits[3], (NDX, NDY, NDZ, 3, F), jnp.float32) ** block_scale(splits[3], (NDX, NDY, NDZ, 3, F), ((0, 4), (1, 4), (2, 2)), -0.2, 0.2), 2.0, 4.0).astype(jnp.bfloat16)
    b_plus = jnp.clip(2.0 + 2.0 * jax.random.uniform(splits[4], (NDX, NDY, NDZ, 3, F), jnp.float32) ** block_scale(splits[4], (NDX, NDY, NDZ, 3, F), ((0, 4), (1, 4), (2, 2)), -0.2, 0.2), 2.0, 4.0).astype(jnp.bfloat16)
    walls = draw_walls(jax.random.fold_in(splits[6], 71), 0)
    return {"w_minus": w_minus, "w_plus": w_plus, "interior": interior, "b_minus": b_minus, "b_plus": b_plus, "walls": walls}


def face_links():
    cells = jnp.arange(F, dtype=jnp.int32)
    rows_u = cells // FSIDE
    rows_v = cells % FSIDE
    apart = jnp.abs(rows_u[:, None] - rows_u[None, :]) + jnp.abs(rows_v[:, None] - rows_v[None, :])
    return (apart == 1).astype(jnp.float32)


def schur_block(factor, inverse, diag_part, links):
    mapped = jnp.dot(inverse, factor, preferred_element_type=jnp.float32).astype(jnp.bfloat16)
    gram = jnp.dot(factor.T, mapped, preferred_element_type=jnp.float32)
    return jnp.diag(diag_part.astype(jnp.float32)) - 0.25 * links - gram


def reference(w_minus, w_plus, interior, b_minus, b_plus, walls):
    links = face_links()

    def one_device(index):
        i = index // (NDY * NDZ)
        j = (index // NDZ) % NDY
        k = index % NDZ
        higher = [(jnp.minimum(i + 1, NDX - 1), j, k), (i, jnp.minimum(j + 1, NDY - 1), k), (i, j, jnp.minimum(k + 1, NDZ - 1))]
        blocks = []
        for axis_id in range(3):
            own = schur_block(w_plus[i, j, k, axis_id], interior[i, j, k], b_plus[i, j, k, axis_id], links)
            ni, nj, nk = higher[axis_id]
            other = schur_block(w_minus[ni, nj, nk, axis_id], interior[ni, nj, nk], b_minus[ni, nj, nk, axis_id], links)
            opened = walls[i, j, k, axis_id] == 0
            total = own + jnp.where(opened, other, jnp.zeros_like(other))
            blocks.append(total.astype(jnp.bfloat16))
        return jnp.stack(blocks)

    result = lax.map(one_device, jnp.arange(NDX * NDY * NDZ, dtype=jnp.int32))
    return result.reshape(NDX, NDY, NDZ, 3, F, F)
```

```python
import functools

import jax
import jax.numpy as jnp
from jax import lax
from jax.experimental import pallas as pl
from jax.experimental.pallas import tpu as pltpu
from jax.sharding import PartitionSpec as P

FSIDE = 32
TILE = 128
STRIP = 256
BF16 = jnp.bfloat16
F32 = jnp.float32
AXES = ("gx", "gy", "gz")


def passed_along(array, axis):
    peers = lax.axis_size(axis)
    return lax.ppermute(array, axis, [(i + 1, i) for i in range(peers - 1)])


def in_vmem(array):
    return pltpu.with_memory_space_constraint(array, pltpu.VMEM)


def params(limit_mib):
    return pltpu.CompilerParams(vmem_limit_bytes=limit_mib << 20)


def spec(space):
    return pl.BlockSpec(memory_space=space)


def starts_of(cols):
    return [sum(cols[:i]) for i in range(len(cols))]


def link_tile(offset):
    p = lax.broadcasted_iota(jnp.int32, (TILE, TILE), 0)
    q = lax.broadcasted_iota(jnp.int32, (TILE, TILE), 1) + offset * TILE
    v = lax.rem(p, FSIDE)
    apart = q - p
    near = (jnp.abs(apart) == FSIDE) | ((apart == 1) & (v != FSIDE - 1)) | ((apart == -1) & (v != 0))
    return near.astype(F32)


def eye_tile():
    p = lax.broadcasted_iota(jnp.int32, (TILE, TILE), 0)
    q = lax.broadcasted_iota(jnp.int32, (TILE, TILE), 1)
    return p == q


def axis_of(turn):
    odd = lax.rem(lax.axis_index("gx"), 2)
    return jnp.where(odd == turn, 2, 1)


def pack_kernel(layout, rank, w_ref, a_ref, b_ref, *refs):
    outs, b_v, sems = refs[:-2], refs[-2], refs[-1]
    width = b_v.shape[1]
    axis_by_turn = [axis_of(turn) for turn in TURNS]
    copies = [pltpu.make_async_copy(b_ref, b_v, sems.at[0])]
    for n, ((turn, start, cols, with_b, with_a), out) in enumerate(zip(layout, outs)):
        axis_id = 0 if turn is None else axis_by_turn[turn]
        copies.append(
            pltpu.make_async_copy(
                w_ref.at[axis_id, :, pl.ds(start, cols)], out.at[pl.ds(0, rank), pl.ds(0, cols)], sems.at[n + 1]
            )
        )
        if with_a:
            copies.append(
                pltpu.make_async_copy(a_ref, out.at[pl.ds(0, rank), pl.ds(cols, rank)], sems.at[len(layout) + 1])
            )
    for copy in copies:
        copy.start()
    copies[0].wait()
    for (turn, start, cols, with_b, with_a), out in zip(layout, outs):
        if with_b:
            diag = b_v[0:1, :]
            if turn is not None:
                diag = jnp.where(axis_by_turn[turn] == 1, b_v[1:2, :], b_v[2:3, :])
            for i in range(0, width, cols):
                n = min(cols, width - i)
                out[rank + i // cols : rank + i // cols + 1, 0:n] = diag[:, i : i + n]
    for copy in copies[1:]:
        copy.wait()


def pack(w, a, b, layout):
    rank = w.shape[1]
    shapes = [(rank + 8 * with_b, cols + rank * with_a) for _, _, cols, with_b, with_a in layout]
    return pl.pallas_call(
        functools.partial(pack_kernel, layout, rank),
        out_shape=[pltpu.VMEM(s, BF16) for s in shapes],
        in_specs=[spec(pl.ANY)] * 3,
        out_specs=[spec(pltpu.VMEM)] * len(shapes),
        scratch_shapes=[pltpu.VMEM(b.shape, BF16), pltpu.SemaphoreType.DMA((len(shapes) + 2,))],
        compiler_params=params(8),
        name="pack",
    )(w, a, b)


def own_kernel(order, walls_hbm, a_ref, w_ref, b_hbm, base_ref, gate_ref, walls_ref, b_ref, a_v, w_v, mapped_v, sems):
    width = w_v.shape[2]
    a_copy = pltpu.make_async_copy(a_ref, a_v, sems.at[len(order)])
    a_copy.start()
    small = [
        pltpu.make_async_copy(walls_hbm, walls_ref, sems.at[len(order) + 1]),
        pltpu.make_async_copy(b_hbm, b_ref, sems.at[len(order) + 2]),
    ]
    for copy in small:
        copy.start()
    copies = []
    for n, axis_id in enumerate(order):
        copy = pltpu.make_async_copy(w_ref.at[axis_id], w_v.at[n], sems.at[n])
        copy.start()
        copies.append(copy)
    links = {offset: link_tile(offset) for offset in (-1, 0, 1)}
    eye = eye_tile()
    for copy in small:
        copy.wait()
    a_copy.wait()
    for n, axis_id in enumerate(order):
        copies[n].wait()
        opened = (walls_ref[axis_id] == 0).astype(F32)
        gate_ref[axis_id] = jnp.full((8, TILE), opened, F32)
        weight = 0.25 + 0.25 * opened
        mapped_v[...] = jnp.dot(a_v[...], w_v[n], preferred_element_type=F32).astype(BF16)
        for r in range(0, width, STRIP):
            base_ref[axis_id, r : r + STRIP, :] = -lax.dot_general(
                w_v[n, :, r : r + STRIP], mapped_v[...], (((0,), (0,)), ((), ())), preferred_element_type=F32
            )
        tiles = width // TILE
        for t in range(tiles):
            rows = pl.ds(t * TILE, TILE)
            for offset in (-1, 0, 1):
                if not 0 <= t + offset < tiles:
                    continue
                cols = pl.ds((t + offset) * TILE, TILE)
                add = -weight * links[offset]
                if offset == 0:
                    diag = b_ref[axis_id : axis_id + 1, t * TILE : (t + 1) * TILE].astype(F32)
                    add = add + jnp.where(eye, diag, 0.0)
                base_ref[axis_id, rows, cols] = base_ref[axis_id, rows, cols] + add


def own(walls, a, w, b, order):
    axes, rank, width = w.shape
    return pl.pallas_call(
        functools.partial(own_kernel, order),
        out_shape=[pltpu.VMEM((axes, width, width), F32), pltpu.VMEM((axes, 8, TILE), F32)],
        in_specs=[spec(pl.ANY)] * 4,
        out_specs=[spec(pltpu.VMEM)] * 2,
        scratch_shapes=[
            pltpu.SMEM(walls.shape, jnp.int32),
            pltpu.VMEM(b.shape, BF16),
            pltpu.VMEM((rank, rank), BF16),
            pltpu.VMEM((len(order), rank, width), BF16),
            pltpu.VMEM((rank, width), BF16),
            pltpu.SemaphoreType.DMA((len(order) + 3,)),
        ],
        compiler_params=params(24),
        cost_estimate=pl.CostEstimate(
            flops=2 * axes * rank * width * (rank + width), bytes_accessed=6 * axes * width * width, transcendentals=0
        ),
        name="own",
    )(walls, a, w, b)


def finish_kernel(turn, rank, cols, news, first, *refs):
    refs = list(refs)
    k = len(cols) - 1
    begin = starts_of(cols)
    s, c = begin[k], cols[k]

    def take(count):
        taken = refs[:count]
        del refs[:count]
        return taken

    gate_ref, base_ref, inverse, with_b = take(4)
    newest, turned, mapped = take(news), take(k), take(k)
    if not first:
        take(1)
    out_ref, fresh, turn_v, stage_col, stage_row, sems = refs
    copies = []

    def send(source, *where):
        copy = pltpu.make_async_copy(source, out_ref.at[where], sems.at[len(copies)])
        copy.start()
        copies.append(copy)

    axis_id = 0 if turn is None else axis_of(turn)
    opened = gate_ref[axis_id, 0:1, 0:1] > 0.5
    new = newest[0][0:rank, 0:c]
    if news > 1:
        new = jnp.concatenate([piece[0:rank, :] for piece in newest], axis=1)
    image = jnp.dot(inverse[0:rank, inverse.shape[1] - rank :], new, preferred_element_type=F32).astype(BF16)
    fresh[...] = jnp.where(opened, image, jnp.zeros_like(image))
    turn_v[...] = new.T
    if k:
        for j in range(k):
            at = slice(begin[j], begin[j] + cols[j])
            gram = jnp.dot(turn_v[...], mapped[j][...], preferred_element_type=F32)
            stage_row[:, at] = (base_ref[axis_id, s : s + c, at] - gram).astype(BF16)
        send(stage_row, axis_id, pl.ds(s, c), pl.ds(0, s))
    b_cols = with_b.shape[1] - (rank if turn is None else 0)
    for j in range(k + 1):
        left = turn_v if j == k else turned[j]
        for r in range(0, cols[j], STRIP):
            e = min(r + STRIP, cols[j])
            gram = jnp.dot(left[r:e, :], fresh[...], preferred_element_type=F32)
            total = base_ref[axis_id, begin[j] + r : begin[j] + e, s : s + c] - gram
            if j == k:
                p = lax.broadcasted_iota(jnp.int32, (e - r, c), 0) + r
                q = lax.broadcasted_iota(jnp.int32, (e - r, c), 1)
                diag = []
                for at in range(s, s + c, TILE):
                    i, start = divmod(at, b_cols)
                    diag.append(with_b[rank + i : rank + i + 1, start : start + TILE].astype(F32))
                diag = jnp.concatenate(diag, axis=1)
                total = total + jnp.where((p == q) & opened, diag, 0.0)
            rows = pl.ds(begin[j] + r, e - r)
            stage_col[rows, :] = total.astype(BF16)
            send(stage_col.at[rows], axis_id, rows, pl.ds(s, c))
    for copy in copies:
        copy.wait()


def finish(gate, base, inverse, with_b, newest, turned, mapped, out, turn, rank, cols, keep):
    axes, width, _ = base.shape
    k = len(cols) - 1
    s, c = starts_of(cols)[k], cols[k]
    first = out is None
    operands = [gate, base, inverse, with_b, *newest, *turned, *mapped]
    specs = [spec(pltpu.VMEM)] * len(operands)
    aliases = {}
    if not first:
        aliases = {len(operands): 0}
        operands.append(out)
        specs.append(spec(pl.ANY))
    kept = [pltpu.VMEM((rank, c), BF16), pltpu.VMEM((c, rank), BF16)]
    scratch = [
        pltpu.VMEM((s + c, c), BF16),
        pltpu.VMEM((c, max(s, TILE)), BF16),
        pltpu.SemaphoreType.DMA((1 + sum(-(-n // STRIP) for n in cols),)),
    ]
    shapes = [jax.ShapeDtypeStruct((axes, width, width), BF16)] + (kept if keep else [])
    return pl.pallas_call(
        functools.partial(finish_kernel, turn, rank, cols, len(newest), first),
        out_shape=shapes,
        in_specs=specs,
        out_specs=[spec(pl.ANY)] + [spec(pltpu.VMEM)] * (len(shapes) - 1),
        scratch_shapes=scratch if keep else kept + scratch,
        input_output_aliases=aliases,
        compiler_params=params(16),
        cost_estimate=pl.CostEstimate(
            flops=2 * rank * c * (rank + 2 * s + c), bytes_accessed=4 * width * c, transcendentals=0
        ),
    )(*operands)


def sends(array, turn):
    if turn is None:
        return passed_along(array, AXES[0])
    nx, ny, nz = (lax.axis_size(axis) for axis in AXES)
    pairs = []
    for i in range(nx):
        for j in range(ny):
            for k in range(nz):
                low = (i * ny + j) * nz + k
                if i % 2 == turn and k + 1 < nz:
                    pairs.append((low + 1, low))
                if i % 2 != turn and j + 1 < ny:
                    pairs.append((low + nz, low))
    return lax.ppermute(array, AXES, pairs)


def in_hbm(array):
    return pltpu.with_memory_space_constraint(array, pltpu.HBM)


TURNS = (0, 1)


def assemble(w_minus, w_plus, interior, b_minus, b_plus, walls):
    _, rank, width = w_plus.shape[3:]
    inverse = interior[0, 0, 0]
    w_minus, w_plus = w_minus[0, 0, 0], w_plus[0, 0, 0]
    b_minus, b_plus, walls = b_minus[0, 0, 0], b_plus[0, 0, 0], walls[0, 0, 0]
    most = width * 3 // 8
    cols = (width // 2, width // 4, width // 4)
    begin = starts_of(cols)

    far = [in_vmem(sends(inverse, turn)) for turn in TURNS]
    layout = [
        ("whole", None, 0, width, True, True),
        ("early", 0, 0, most, False, False),
        ("late", 0, most, width - most, True, False),
    ]
    layout += [(f"piece{k}", 1, begin[k], cols[k], k == 0, False) for k in range(len(cols))]
    packed = pack(in_hbm(w_minus), in_hbm(inverse), in_hbm(b_minus), [entry[1:] for entry in layout])
    whole, early, late, *pieces = [in_vmem(sends(p, entry[1])) for p, entry in zip(packed, layout)]
    base, gate = own(in_hbm(walls), in_hbm(inverse), in_hbm(w_plus), in_hbm(b_plus), (2, 1, 0))
    base, gate = in_vmem(base), in_vmem(gate)

    (out,) = finish(gate, base, whole, whole, [whole], [], [], None, None, rank, (width,), False)
    (out,) = finish(gate, base, far[0], late, [early, late], [], [], out, 0, rank, (width,), False)
    turned, mapped = [], []
    for k in range(len(cols)):
        out, *kept = finish(
            gate, base, far[1], pieces[0], pieces[k : k + 1], turned, mapped, out, 1, rank, cols[: k + 1],
            k + 1 < len(cols),
        )
        if kept:
            mapped = mapped + [in_vmem(kept[0])]
            turned = turned + [in_vmem(kept[1])]
    return out[None, None, None]


def solution(mesh):
    in_specs = (
        P("gx", "gy", "gz", None, None, None),
        P("gx", "gy", "gz", None, None, None),
        P("gx", "gy", "gz", None, None),
        P("gx", "gy", "gz", None, None),
        P("gx", "gy", "gz", None, None),
        P("gx", "gy", "gz", None),
    )
    out_specs = P("gx", "gy", "gz", None, None, None)
    return jax.shard_map(assemble, mesh=mesh, in_specs=in_specs, out_specs=out_specs, check_vma=False)
```

```python
import functools

import jax
import jax.numpy as jnp
from jax import lax
from jax.experimental import pallas as pl
from jax.experimental.pallas import tpu as pltpu
from jax.sharding import PartitionSpec as P

FSIDE = 32
TILE = 128
STRIP = 256
BF16 = jnp.bfloat16
F32 = jnp.float32
AXES = ("gx", "gy", "gz")


def passed_along(array, axis):
    peers = lax.axis_size(axis)
    return lax.ppermute(array, axis, [(i + 1, i) for i in range(peers - 1)])


def in_vmem(array):
    return pltpu.with_memory_space_constraint(array, pltpu.VMEM)


def params(limit_mib):
    return pltpu.CompilerParams(vmem_limit_bytes=limit_mib << 20)


def spec(space):
    return pl.BlockSpec(memory_space=space)


def starts_of(cols):
    return [sum(cols[:i]) for i in range(len(cols))]


def link_tile(offset):
    p = lax.broadcasted_iota(jnp.int32, (TILE, TILE), 0)
    q = lax.broadcasted_iota(jnp.int32, (TILE, TILE), 1) + offset * TILE
    v = lax.rem(p, FSIDE)
    apart = q - p
    near = (jnp.abs(apart) == FSIDE) | ((apart == 1) & (v != FSIDE - 1)) | ((apart == -1) & (v != 0))
    return near.astype(F32)


def eye_tile():
    p = lax.broadcasted_iota(jnp.int32, (TILE, TILE), 0)
    q = lax.broadcasted_iota(jnp.int32, (TILE, TILE), 1)
    return p == q


def axis_of(turn):
    odd = lax.rem(lax.axis_index("gx"), 2)
    return jnp.where(odd == turn, 2, 1)


def pack_kernel(layout, rank, w_ref, a_ref, b_ref, *refs):
    outs, b_v, sems = refs[:-2], refs[-2], refs[-1]
    width = b_v.shape[1]
    axis_by_turn = [axis_of(turn) for turn in TURNS]
    copies = [pltpu.make_async_copy(b_ref, b_v, sems.at[0])]
    for n, ((turn, start, cols, with_b, with_a), out) in enumerate(zip(layout, outs)):
        axis_id = 0 if turn is None else axis_by_turn[turn]
        copies.append(
            pltpu.make_async_copy(
                w_ref.at[axis_id, :, pl.ds(start, cols)], out.at[pl.ds(0, rank), pl.ds(0, cols)], sems.at[n + 1]
            )
        )
        if with_a:
            copies.append(
                pltpu.make_async_copy(a_ref, out.at[pl.ds(0, rank), pl.ds(cols, rank)], sems.at[len(layout) + 1])
            )
    for copy in copies:
        copy.start()
    copies[0].wait()
    for (turn, start, cols, with_b, with_a), out in zip(layout, outs):
        if with_b:
            diag = b_v[0:1, :]
            if turn is not None:
                diag = jnp.where(axis_by_turn[turn] == 1, b_v[1:2, :], b_v[2:3, :])
            for i in range(0, width, cols):
                n = min(cols, width - i)
                out[rank + i // cols : rank + i // cols + 1, 0:n] = diag[:, i : i + n]
    for copy in copies[1:]:
        copy.wait()


def pack(w, a, b, layout):
    rank = w.shape[1]
    shapes = [(rank + 8 * with_b, cols + rank * with_a) for _, _, cols, with_b, with_a in layout]
    return pl.pallas_call(
        functools.partial(pack_kernel, layout, rank),
        out_shape=[pltpu.VMEM(s, BF16) for s in shapes],
        in_specs=[spec(pl.ANY)] * 3,
        out_specs=[spec(pltpu.VMEM)] * len(shapes),
        scratch_shapes=[pltpu.VMEM(b.shape, BF16), pltpu.SemaphoreType.DMA((len(shapes) + 2,))],
        compiler_params=params(8),
        name="pack",
    )(w, a, b)


def own_kernel(order, walls_hbm, a_ref, w_ref, b_hbm, base_ref, gate_ref, walls_ref, b_ref, a_v, w_v, mapped_v, sems):
    width = w_v.shape[2]
    a_copy = pltpu.make_async_copy(a_ref, a_v, sems.at[len(order)])
    a_copy.start()
    small = [
        pltpu.make_async_copy(walls_hbm, walls_ref, sems.at[len(order) + 1]),
        pltpu.make_async_copy(b_hbm, b_ref, sems.at[len(order) + 2]),
    ]
    for copy in small:
        copy.start()
    copies = []
    for n, axis_id in enumerate(order):
        copy = pltpu.make_async_copy(w_ref.at[axis_id], w_v.at[n], sems.at[n])
        copy.start()
        copies.append(copy)
    links = {offset: link_tile(offset) for offset in (-1, 0, 1)}
    eye = eye_tile()
    for copy in small:
        copy.wait()
    a_copy.wait()
    for n, axis_id in enumerate(order):
        copies[n].wait()
        opened = (walls_ref[axis_id] == 0).astype(F32)
        gate_ref[axis_id] = jnp.full((8, TILE), opened, F32)
        weight = 0.25 + 0.25 * opened
        mapped_v[...] = jnp.dot(a_v[...], w_v[n], preferred_element_type=F32).astype(BF16)
        for r in range(0, width, STRIP):
            base_ref[axis_id, r : r + STRIP, :] = -lax.dot_general(
                w_v[n, :, r : r + STRIP], mapped_v[...], (((0,), (0,)), ((), ())), preferred_element_type=F32
            )
        tiles = width // TILE
        for t in range(tiles):
            rows = pl.ds(t * TILE, TILE)
            for offset in (-1, 0, 1):
                if not 0 <= t + offset < tiles:
                    continue
                cols = pl.ds((t + offset) * TILE, TILE)
                add = -weight * links[offset]
                if offset == 0:
                    diag = b_ref[axis_id : axis_id + 1, t * TILE : (t + 1) * TILE].astype(F32)
                    add = add + jnp.where(eye, diag, 0.0)
                base_ref[axis_id, rows, cols] = base_ref[axis_id, rows, cols] + add


def own(walls, a, w, b, order):
    axes, rank, width = w.shape
    return pl.pallas_call(
        functools.partial(own_kernel, order),
        out_shape=[pltpu.VMEM((axes, width, width), F32), pltpu.VMEM((axes, 8, TILE), F32)],
        in_specs=[spec(pl.ANY)] * 4,
        out_specs=[spec(pltpu.VMEM)] * 2,
        scratch_shapes=[
            pltpu.SMEM(walls.shape, jnp.int32),
            pltpu.VMEM(b.shape, BF16),
            pltpu.VMEM((rank, rank), BF16),
            pltpu.VMEM((len(order), rank, width), BF16),
            pltpu.VMEM((rank, width), BF16),
            pltpu.SemaphoreType.DMA((len(order) + 3,)),
        ],
        compiler_params=params(24),
        cost_estimate=pl.CostEstimate(
            flops=2 * axes * rank * width * (rank + width), bytes_accessed=6 * axes * width * width, transcendentals=0
        ),
        name="own",
    )(walls, a, w, b)


def finish_kernel(turn, rank, cols, news, first, *refs):
    refs = list(refs)
    k = len(cols) - 1
    begin = starts_of(cols)
    s, c = begin[k], cols[k]

    def take(count):
        taken = refs[:count]
        del refs[:count]
        return taken

    gate_ref, base_ref, inverse, with_b = take(4)
    newest, turned, mapped = take(news), take(k), take(k)
    if not first:
        take(1)
    out_ref, fresh, turn_v, stage_col, stage_row, sems = refs
    copies = []

    def send(source, *where):
        copy = pltpu.make_async_copy(source, out_ref.at[where], sems.at[len(copies)])
        copy.start()
        copies.append(copy)

    axis_id = 0 if turn is None else axis_of(turn)
    opened = gate_ref[axis_id, 0:1, 0:1] > 0.5
    new = newest[0][0:rank, 0:c]
    if news > 1:
        new = jnp.concatenate([piece[0:rank, :] for piece in newest], axis=1)
    image = jnp.dot(inverse[0:rank, inverse.shape[1] - rank :], new, preferred_element_type=F32).astype(BF16)
    fresh[...] = jnp.where(opened, image, jnp.zeros_like(image))
    turn_v[...] = new.T
    if k:
        for j in range(k):
            at = slice(begin[j], begin[j] + cols[j])
            gram = jnp.dot(turn_v[...], mapped[j][...], preferred_element_type=F32)
            stage_row[:, at] = (base_ref[axis_id, s : s + c, at] - gram).astype(BF16)
        send(stage_row, axis_id, pl.ds(s, c), pl.ds(0, s))
    b_cols = with_b.shape[1] - (rank if turn is None else 0)
    for j in range(k + 1):
        left = turn_v if j == k else turned[j]
        for r in range(0, cols[j], STRIP):
            e = min(r + STRIP, cols[j])
            gram = jnp.dot(left[r:e, :], fresh[...], preferred_element_type=F32)
            total = base_ref[axis_id, begin[j] + r : begin[j] + e, s : s + c] - gram
            if j == k:
                p = lax.broadcasted_iota(jnp.int32, (e - r, c), 0) + r
                q = lax.broadcasted_iota(jnp.int32, (e - r, c), 1)
                diag = []
                for at in range(s, s + c, TILE):
                    i, start = divmod(at, b_cols)
                    diag.append(with_b[rank + i : rank + i + 1, start : start + TILE].astype(F32))
                diag = jnp.concatenate(diag, axis=1)
                total = total + jnp.where((p == q) & opened, diag, 0.0)
            rows = pl.ds(begin[j] + r, e - r)
            stage_col[rows, :] = total.astype(BF16)
            send(stage_col.at[rows], axis_id, rows, pl.ds(s, c))
    for copy in copies:
        copy.wait()


def finish(gate, base, inverse, with_b, newest, turned, mapped, out, turn, rank, cols, keep):
    axes, width, _ = base.shape
    k = len(cols) - 1
    s, c = starts_of(cols)[k], cols[k]
    first = out is None
    operands = [gate, base, inverse, with_b, *newest, *turned, *mapped]
    specs = [spec(pltpu.VMEM)] * len(operands)
    aliases = {}
    if not first:
        aliases = {len(operands): 0}
        operands.append(out)
        specs.append(spec(pl.ANY))
    kept = [pltpu.VMEM((rank, c), BF16), pltpu.VMEM((c, rank), BF16)]
    scratch = [
        pltpu.VMEM((s + c, c), BF16),
        pltpu.VMEM((c, max(s, TILE)), BF16),
        pltpu.SemaphoreType.DMA((1 + sum(-(-n // STRIP) for n in cols),)),
    ]
    shapes = [jax.ShapeDtypeStruct((axes, width, width), BF16)] + (kept if keep else [])
    return pl.pallas_call(
        functools.partial(finish_kernel, turn, rank, cols, len(newest), first),
        out_shape=shapes,
        in_specs=specs,
        out_specs=[spec(pl.ANY)] + [spec(pltpu.VMEM)] * (len(shapes) - 1),
        scratch_shapes=scratch if keep else kept + scratch,
        input_output_aliases=aliases,
        compiler_params=params(16),
        cost_estimate=pl.CostEstimate(
            flops=2 * rank * c * (rank + 2 * s + c), bytes_accessed=4 * width * c, transcendentals=0
        ),
    )(*operands)


def sends(array, turn):
    if turn is None:
        return passed_along(array, AXES[0])
    nx, ny, nz = (lax.axis_size(axis) for axis in AXES)
    pairs = []
    for i in range(nx):
        for j in range(ny):
            for k in range(nz):
                low = (i * ny + j) * nz + k
                if i % 2 == turn and k + 1 < nz:
                    pairs.append((low + 1, low))
                if i % 2 != turn and j + 1 < ny:
                    pairs.append((low + nz, low))
    return lax.ppermute(array, AXES, pairs)


def in_hbm(array):
    return pltpu.with_memory_space_constraint(array, pltpu.HBM)


TURNS = (0, 1)


def assemble(w_minus, w_plus, interior, b_minus, b_plus, walls):
    _, rank, width = w_plus.shape[3:]
    inverse = interior[0, 0, 0]
    w_minus, w_plus = w_minus[0, 0, 0], w_plus[0, 0, 0]
    b_minus, b_plus, walls = b_minus[0, 0, 0], b_plus[0, 0, 0], walls[0, 0, 0]
    most = width // 4
    cols = (width * 3 // 8, width * 3 // 8, width // 4)
    begin = starts_of(cols)

    far = [in_vmem(sends(inverse, turn)) for turn in TURNS]
    layout = [
        ("whole", None, 0, width, True, True),
        ("early", 0, 0, most, True, False),
        ("late", 0, most, width - most, False, False),
    ]
    layout += [(f"piece{k}", 1, begin[k], cols[k], k == 0, False) for k in range(len(cols))]
    packed = pack(in_hbm(w_minus), in_hbm(inverse), in_hbm(b_minus), [entry[1:] for entry in layout])
    whole, early, late, *pieces = [in_vmem(sends(p, entry[1])) for p, entry in zip(packed, layout)]
    base, gate = own(in_hbm(walls), in_hbm(inverse), in_hbm(w_plus), in_hbm(b_plus), (2, 1, 0))
    base, gate = in_vmem(base), in_vmem(gate)

    (out,) = finish(gate, base, whole, whole, [whole], [], [], None, None, rank, (width,), False)
    (out,) = finish(gate, base, far[0], early, [early, late], [], [], out, 0, rank, (width,), False)
    turned, mapped = [], []
    for k in range(len(cols)):
        out, *kept = finish(
            gate, base, far[1], pieces[0], pieces[k : k + 1], turned, mapped, out, 1, rank, cols[: k + 1],
            k + 1 < len(cols),
        )
        if kept:
            mapped = mapped + [in_vmem(kept[0])]
            turned = turned + [in_vmem(kept[1])]
    return out[None, None, None]


def solution(mesh):
    in_specs = (
        P("gx", "gy", "gz", None, None, None),
        P("gx", "gy", "gz", None, None, None),
        P("gx", "gy", "gz", None, None),
        P("gx", "gy", "gz", None, None),
        P("gx", "gy", "gz", None, None),
        P("gx", "gy", "gz", None),
    )
    out_specs = P("gx", "gy", "gz", None, None, None)
    return jax.shard_map(assemble, mesh=mesh, in_specs=in_specs, out_specs=out_specs, check_vma=False)
```
